256 devices in a mesh: dp: 4 (over x), expert: 64 (over y, z, core).
Axes of the slice: x: 4, y: 4, z: 8, core: 2. Of those that a mesh axis runs over, the one named last changes fastest.
Arguments:
- tokens: bfloat16 [8192, 4096], P('expert', 'dp'), may hold values from -6 to 6
- routes: int32 [8192, 4], P('expert'), may hold values from 0 to 63, all different within a row; in each aligned block of 128 rows (0 to 127, 128 to 255, ...) at most 16 rows name the same one
- route_weights: float32 [8192, 4], P('expert'), may hold values from 0.1 to 1
- gate_weight: bfloat16 [64, 4096, 1536], P('expert', None, 'dp'), may hold values from -0.09375 to 0.09375
- up_weight: bfloat16 [64, 4096, 1536], P('expert', None, 'dp'), may hold values from -0.09375 to 0.09375
- down_weight: bfloat16 [64, 1536, 4096], P('expert', 'dp'), may hold values from -0.15625 to 0.15625
- sketch_basis: bfloat16 [1536, 128], P('dp'), may hold values from -0.15625 to 0.15625
Outputs:
- mixed: bfloat16 [8192, 4096], P('expert', 'dp')
- sketch: float32 [64, 128, 1536], P('expert', None, 'dp')
The draws below stay inside these ranges and needn't reach their ends.
Inputs may be any that keep to these rules, and one draw needn't show every extreme that they name: `routes`: each row names 4 different experts; within the rows of one device no expert is named more than 16 times, a bound that some block reaches.
All inputs are finite; a program needn't handle non-finite values.
Results may differ from the reference program's by a relative error of at most 0.017.
Values may be sent and summed in bfloat16 or wider, within the bound.
No kernel may reach another device: no remote copies, remote signals or barrier semaphores. Data moves between devices by JAX's collectives and lax.ppermute only.
A program may use at most 128 MiB of HBM per device.

```python
import math
import jax
import jax.numpy as jnp
import numpy as np
from jax import lax

D = 4096
FF = 1536
TOP = 4
SK = 128
TOK_DEV = 128
EXPERTS = 64
FF_DEV = 384
CAP = 16
TOKENS = 8192
N_DP = 4
N_EXPERT = 64


def level_of(rng, shape, shards, low, high):
    factor_of = 1.0
    for axis_at, blocks in shards:
        steps = jax.random.uniform(jax.random.fold_in(jax.random.fold_in(rng, 6), axis_at), (blocks,), jnp.float32, low / len(shards), high / len(shards))
        factor_of = factor_of * jnp.repeat(jnp.exp(steps), shape[axis_at] // blocks).reshape((-1,) + (1,) * (len(shape) - 1 - axis_at))
    return factor_of


def routed_block(rng, own, number, rows, number_of, top, bound, skew):
    ranking = jax.random.permutation(rng, number_of)
    heavy_load, common = load_shares(number_of, rows * top, bound, skew, True), load_shares(number_of, rows * top, bound, skew, False)
    places = jnp.arange(number_of)

    def named(sizes, turn):
        used = int((sizes > 0).sum())
        fixed = max(1, used // 4)
        passed = fixed + (places - fixed + turn * (used - fixed)) % max(1, number_of - fixed)
        return jnp.zeros((number_of,), jnp.int32).at[ranking[jnp.where(places < fixed, places, passed)]].set(jnp.asarray(sizes, jnp.int32))

    sizes = jnp.where(number % 4 == 0, named(heavy_load, number // 4), named(common, number - number // 4 - 1))
    mixed = jax.random.permutation(jax.random.fold_in(own, 3), number_of)
    source_of, taker = mixed[0:number_of // 2 * 2:2], mixed[1:number_of // 2 * 2:2]
    slack = jnp.minimum(sizes[source_of] - 1, bound - sizes[taker]) // 2
    slack = jnp.where((source_of == ranking[0]) | (taker == ranking[0]) | (sizes[taker] == 0), 0, jnp.maximum(slack, 0))
    passed = jax.random.randint(jax.random.fold_in(own, 4), (number_of // 2,), 0, 1 << 20) % (slack + 1)
    sizes = sizes.at[source_of].add(-passed).at[taker].add(passed)
    members = jnp.searchsorted(jnp.cumsum(sizes), jnp.arange(rows * top), side="right").astype(jnp.int32)
    table = members.reshape(top, rows).T
    table = table[jax.random.permutation(jax.random.fold_in(own, 1), rows)]
    turn = jax.random.randint(jax.random.fold_in(own, 2), (rows, 1), 0, top)
    return jnp.take_along_axis(table, (jnp.arange(top)[None, :] + turn) % top, axis=1)


def load_shares(number_of, total, limit, slope, full):
    portions = [(1 << 20) // math.isqrt(standing ** slope) + 1 for standing in range(1, number_of + 1)]
    largest = limit if full else min(limit, max(-(-total // number_of), total * portions[0] // sum(portions)))
    least = 1 if total - largest >= number_of - 1 else 0
    holding, spare = [largest] + [least] * (number_of - 1), total - largest - least * (number_of - 1)
    while spare > 0:
        candidates = [i for i in range(1, number_of) if holding[i] < largest] or [i for i in range(1, number_of) if holding[i] < limit]
        mass, remaining = sum([portions[i] for i in candidates]), spare
        for i in candidates:
            extra = min(limit - holding[i], max(1, remaining * portions[i] // mass), spare)
            holding[i] = holding[i] + extra
            spare = spare - extra
    return np.array(holding)


def normal_values(rng, shape, deviation, bound, split=(), kind=jnp.bfloat16):
    level = level_of(rng, shape, split, -0.22, 0.18) if split else 1.0
    entries = jax.random.normal(rng, shape, jnp.float32) * deviation * level
    return jnp.minimum(jnp.maximum(entries, -bound), bound).astype(kind)


def setup_inputs(seed: int = 0) -> dict:
    key_of = jax.random.split(jax.random.key(seed), 8)
    tokens = normal_values(key_of[0], (TOKENS, D), 1.0, 6.0, ((0, 64), (1, 4)))
    routes_keys = jax.random.split(jax.random.fold_in(key_of[1], 1), TOKENS // TOK_DEV)
    routes_turns = jax.random.permutation(jax.random.fold_in(key_of[1], 3), TOKENS // TOK_DEV)
    routes = jax.vmap(lambda own, number: routed_block(jax.random.fold_in(key_of[1], 2), own, number, TOK_DEV, EXPERTS, TOP, CAP, 2))(routes_keys, routes_turns).reshape((TOKENS, TOP))
    route_weights = jnp.clip(0.1 + 0.9 * jax.random.uniform(key_of[2], (TOKENS, TOP), jnp.float32) ** level_of(key_of[2], (TOKENS, TOP), ((0, 64),), -0.2, 0.2), 0.1, 1.0)
    gate_weight = normal_values(key_of[3], (EXPERTS, D, FF), D ** -0.5, 0.09375, ((0, 64), (2, 4)))
    up_weight = normal_values(key_of[4], (EXPERTS, D, FF), D ** -0.5, 0.09375, ((0, 64), (2, 4)))
    down_weight = normal_values(key_of[5], (EXPERTS, FF, D), FF ** -0.5, 0.15625, ((0, 64), (1, 4)))
    sketch_basis = normal_values(key_of[6], (FF, SK), FF ** -0.5, 0.15625, ((0, 4),))
    return {"tokens": tokens, "routes": routes, "route_weights": route_weights, "gate_weight": gate_weight, "up_weight": up_weight, "down_weight": down_weight, "sketch_basis": sketch_basis}


ridge_term = 1.0

def reference(tokens, routes, route_weights, gate_weight, up_weight, down_weight, sketch_basis):
    route_list = routes.reshape(-1)
    order_list = jnp.argsort(route_list, stable=True).astype(jnp.int32)
    row_limit = N_EXPERT * CAP
    padded_order = jnp.concatenate([order_list, jnp.zeros((row_limit,), jnp.int32)])
    onehot = (route_list[:, None] == jnp.arange(EXPERTS, dtype=jnp.int32)[None, :]).astype(jnp.int32)
    expert_counts = jnp.sum(onehot, axis=0).astype(jnp.int32)
    expert_starts = (jnp.cumsum(expert_counts) - expert_counts).astype(jnp.int32)
    weight_list = route_weights.reshape(-1)
    block_rows = min(256, row_limit)
    eye_matrix = jnp.eye(SK, dtype=jnp.float32)

    def per_expert(accum, inputs):
        begin_at, live_total, gate_expert, up_expert, down_expert = inputs
        pair_rows = lax.dynamic_slice_in_dim(padded_order, begin_at, row_limit, 0)

        def one_block(block_index, state):
            mixed_acc, gram_acc, proj_acc = state
            offset = block_index * block_rows
            pair_block = lax.dynamic_slice_in_dim(pair_rows, offset, block_rows, 0)
            alive = offset + jnp.arange(block_rows, dtype=jnp.int32) < live_total
            token_ids = pair_block // TOP
            chosen = jnp.where(alive[:, None], tokens[token_ids], jnp.zeros((), tokens.dtype))
            gate_val = jnp.dot(chosen.astype(jnp.float32), gate_expert.astype(jnp.float32), preferred_element_type=jnp.float32)
            up_val = jnp.dot(chosen.astype(jnp.float32), up_expert.astype(jnp.float32), preferred_element_type=jnp.float32)
            hidden = (jax.nn.silu(gate_val) * up_val).astype(jnp.bfloat16)
            summed = jnp.zeros((block_rows, D), jnp.float32)
            for quarter in range(N_DP):
                lower_unit = quarter * FF_DEV
                part = jnp.dot(hidden[:, lower_unit:lower_unit + FF_DEV].astype(jnp.float32), down_expert[lower_unit:lower_unit + FF_DEV, :].astype(jnp.float32), preferred_element_type=jnp.float32).astype(jnp.bfloat16)
                summed = summed + part.astype(jnp.float32)
            expert_out = summed.astype(jnp.bfloat16)
            pair_weight = jnp.where(alive, weight_list[pair_block], 0.0)
            mixed_acc = mixed_acc.at[token_ids].add(pair_weight[:, None] * expert_out.astype(jnp.float32))
            sketch_rows = jnp.dot(hidden.astype(jnp.float32), sketch_basis.astype(jnp.float32), preferred_element_type=jnp.float32)
            gram_acc = gram_acc + jnp.dot(sketch_rows.T, sketch_rows, precision=lax.Precision.HIGHEST)
            proj_acc = proj_acc + jnp.dot(sketch_rows.T, hidden.astype(jnp.float32), precision=lax.Precision.HIGHEST)
            return (mixed_acc, gram_acc, proj_acc)
        block_count = (live_total + block_rows - 1) // block_rows
        start_state = (accum, jnp.zeros((SK, SK), jnp.float32), jnp.zeros((SK, FF), jnp.float32))
        accum, gram_total, proj_total = lax.fori_loop(0, block_count, one_block, start_state)
        lower_factor = jnp.linalg.cholesky(gram_total + ridge_term * eye_matrix)
        whitened = jax.scipy.linalg.solve_triangular(lower_factor, proj_total, lower=True)
        return (accum, whitened)
    start_accum = jnp.zeros((TOKENS, D), jnp.float32)
    mixed_total, sketches = lax.scan(per_expert, start_accum, (expert_starts, expert_counts, gate_weight, up_weight, down_weight))
    return (mixed_total.astype(jnp.bfloat16), sketches)
```

```python
import functools

import jax
import jax.numpy as jnp
from jax import lax
from jax.experimental import pallas as pl
from jax.experimental.pallas import tpu as pltpu
from jax.sharding import PartitionSpec as P

ridge_term = 1.0
SLOT_CHUNKS = 1
VMEM = pl.BlockSpec(memory_space=pltpu.VMEM)


def slot_codes(routes, experts):
    tokens, top = routes.shape
    expert_of = lax.broadcasted_iota(jnp.int32, (tokens, experts), 1)
    hits = [(routes[:, k : k + 1] == expert_of).astype(jnp.float32) for k in range(top)]
    hit = functools.reduce(jnp.add, hits)
    row = lax.broadcasted_iota(jnp.int32, (tokens, tokens), 0)
    column = lax.broadcasted_iota(jnp.int32, (tokens, tokens), 1)
    earlier = (row > column).astype(jnp.bfloat16)
    before = jnp.dot(earlier, hit.astype(jnp.bfloat16), preferred_element_type=jnp.float32)
    return hits, jnp.where(hit > 0.0, before, -1.0)


def spread(values, experts, slots):
    expert = lax.broadcasted_iota(jnp.int32, (experts, experts * slots), 0)
    first = expert * slots
    at = lax.broadcasted_iota(jnp.int32, (experts, experts * slots), 1)
    ones = jnp.where((at >= first) & (at < first + slots), 1.0, 0.0).astype(jnp.bfloat16)
    return jnp.dot(values.astype(jnp.bfloat16), ones, preferred_element_type=jnp.float32)


def slot_numbers(tokens, experts, slots, start):
    at = lax.broadcasted_iota(jnp.int32, (tokens, experts * slots), 1)
    return (lax.rem(at, slots) + start).astype(jnp.float32)


def dispatch_kernel(experts, slots, routes_ref, tokens_ref, *out_refs):
    _, code = slot_codes(routes_ref[...], experts)
    tokens = tokens_ref[...]
    wide = spread(code, experts, slots)
    for chunk, out_ref in enumerate(out_refs):
        numbers = slot_numbers(tokens.shape[0], experts, slots, chunk * slots)
        chosen = jnp.where(wide == numbers, 1.0, 0.0).T.astype(jnp.bfloat16)
        out_ref[...] = jnp.dot(chosen, tokens, preferred_element_type=jnp.float32).astype(out_ref.dtype)


def dispatch(routes, tokens, experts, slots, chunks):
    rows, width = experts * slots, tokens.shape[1]
    return pl.pallas_call(
        functools.partial(dispatch_kernel, experts, slots),
        out_shape=[jax.ShapeDtypeStruct((rows, width), tokens.dtype)] * chunks,
        in_specs=[VMEM] * 2,
        out_specs=[VMEM] * chunks,
        name="dispatch",
    )(routes, tokens)


def combine_kernel(experts, slots, routes_ref, weights_ref, *refs):
    out_ref = refs[-1]
    hits, code = slot_codes(routes_ref[...], experts)
    weights = weights_ref[...]
    weight = functools.reduce(jnp.add, [h * weights[:, k : k + 1] for k, h in enumerate(hits)])
    high = weight.astype(jnp.bfloat16)
    low = (weight - high.astype(jnp.float32)).astype(jnp.bfloat16)
    wide = spread(code, experts, slots)
    high_wide = spread(high, experts, slots)
    low_wide = spread(low, experts, slots)
    total = None
    for chunk, row_ref in enumerate(refs[:-1]):
        numbers = slot_numbers(weight.shape[0], experts, slots, chunk * slots)
        chosen = wide == numbers
        rows = row_ref[...]
        for part in (high_wide, low_wide):
            matrix = jnp.where(chosen, part, 0.0).astype(jnp.bfloat16)
            term = jnp.dot(matrix, rows, preferred_element_type=jnp.float32)
            total = term if total is None else total + term
    out_ref[...] = total.astype(out_ref.dtype)


def combine(routes, weights, rows, experts, slots):
    return pl.pallas_call(
        functools.partial(combine_kernel, experts, slots),
        out_shape=jax.ShapeDtypeStruct((routes.shape[0], rows[0].shape[1]), jnp.bfloat16),
        in_specs=[VMEM] * (2 + len(rows)),
        out_specs=VMEM,
        name="combine",
    )(routes, weights, *rows)


def hidden_kernel(rows_ref, gate_ref, up_ref, *refs):
    hidden_ref = refs[-1]
    parts, block, width = rows_ref.shape
    gate = up = None
    for part in range(parts):
        rows = rows_ref[part]
        cut = pl.ds(part * width, width)
        gate_term = jnp.dot(rows, gate_ref[cut, :], preferred_element_type=jnp.float32)
        up_term = jnp.dot(rows, up_ref[cut, :], preferred_element_type=jnp.float32)
        gate = gate_term if gate is None else gate + gate_term
        up = up_term if up is None else up + up_term
    at = pl.multiple_of(pl.program_id(0) * block, block)
    hidden_ref[pl.ds(at, block), :] = (gate / (1.0 + jnp.exp(-gate)) * up).astype(hidden_ref.dtype)
    for extra_ref in refs[:-1]:
        count = hidden_ref.shape[0] - extra_ref.shape[0]

        @pl.when(pl.program_id(0) == 0)
        def _():
            hidden_ref[count:, :] = extra_ref[...]


def hidden_of(rows, gate_weight, up_weight, extra):
    parts, count, width = rows.shape
    units = gate_weight.shape[1]
    block = min(256, count)
    whole = pl.BlockSpec(gate_weight.shape, lambda i: (0, 0))
    total = count + sum(e.shape[0] for e in extra)
    return pl.pallas_call(
        hidden_kernel,
        grid=(count // block,),
        out_shape=jax.ShapeDtypeStruct((total, units), jnp.bfloat16),
        in_specs=[pl.BlockSpec((parts, block, width), lambda i: (0, i, 0)), whole, whole]
        + [pl.BlockSpec(e.shape, lambda i: (0, 0)) for e in extra],
        out_specs=pl.BlockSpec((total, units), lambda i: (0, 0)),
        cost_estimate=pl.CostEstimate(
            flops=4 * parts * count * width * units,
            bytes_accessed=2 * parts * width * (count + 2 * units) + 2 * count * units,
            transcendentals=count * units,
        ),
        compiler_params=pltpu.CompilerParams(vmem_limit_bytes=48 << 20),
        name="hidden",
    )(rows, gate_weight, up_weight, *extra)


def output_kernel(me_ref, hidden_ref, *refs):
    out_ref = refs[-1]
    parts = hidden_ref.shape[0]
    total = None
    for shift, down_ref in enumerate(refs[:-1]):
        part = lax.rem(me_ref[0] + parts - shift, parts)
        term = jnp.dot(hidden_ref[part], down_ref[...], preferred_element_type=jnp.float32)
        total = term if total is None else total + term
    out_ref[...] = total.astype(out_ref.dtype)


def output_of(hidden, down, count):
    parts, _, units = hidden.shape
    width = down[0].shape[1]
    block = min(256, count)
    me = lax.axis_index("dp").astype(jnp.int32).reshape(1)
    return pl.pallas_call(
        output_kernel,
        grid_spec=pltpu.PrefetchScalarGridSpec(
            num_scalar_prefetch=1,
            grid=(count // block,),
            in_specs=[pl.BlockSpec((parts, block, units), lambda i, me: (0, i, 0))]
            + [pl.BlockSpec(d.shape, lambda i, me: (0, 0)) for d in down],
            out_specs=pl.BlockSpec((block, width), lambda i, me: (i, 0)),
        ),
        out_shape=jax.ShapeDtypeStruct((count, width), jnp.bfloat16),
        cost_estimate=pl.CostEstimate(
            flops=2 * parts * count * width * units,
            bytes_accessed=2 * parts * units * (count + width) + 2 * count * width,
            transcendentals=0,
        ),
        compiler_params=pltpu.CompilerParams(vmem_limit_bytes=48 << 20),
        name="output",
    )(me, hidden, *down)


def moments_kernel(chunks, count, *refs):
    gram_ref, project_ref = refs[-2:]
    first_ref = refs[0]
    gram = project = None
    for full_ref, own_ref in zip(refs[:chunks], refs[chunks : 2 * chunks]):
        rows = None
        for part in range(full_ref.shape[0]):
            basis = first_ref[part, count:, :]
            term = lax.dot_general(
                full_ref[part, :count, :],
                basis,
                (((1,), (1,)), ((), ())),
                preferred_element_type=jnp.float32,
            )
            rows = term if rows is None else rows + term
        turned = rows.T
        own = own_ref[:count, :].astype(jnp.float32)
        gram_term = jnp.dot(
            turned, rows, precision=lax.Precision.HIGHEST, preferred_element_type=jnp.float32
        )
        project_term = jnp.dot(
            turned, own, precision=lax.Precision.HIGHEST, preferred_element_type=jnp.float32
        )
        gram = gram_term if gram is None else gram + gram_term
        project = project_term if project is None else project + project_term
    size = gram.shape[0]
    row = lax.broadcasted_iota(jnp.int32, (size, size), 0)
    column = lax.broadcasted_iota(jnp.int32, (size, size), 1)
    gram_ref[...] = gram + jnp.where(row == column, ridge_term, 0.0)
    project_ref[...] = project


def moments(full, own, count, size):
    units = own[0].shape[1]
    return pl.pallas_call(
        functools.partial(moments_kernel, len(full), count),
        out_shape=[
            jax.ShapeDtypeStruct((size, size), jnp.float32),
            jax.ShapeDtypeStruct((size, units), jnp.float32),
        ],
        in_specs=[VMEM] * (2 * len(full)),
        out_specs=[VMEM] * 2,
        compiler_params=pltpu.CompilerParams(vmem_limit_bytes=48 << 20),
        name="moments",
    )(*full, *own)


def turn_down(down_weight, width):
    splits, me = lax.axis_size("dp"), lax.axis_index("dp")
    pieces = []
    for shift in range(splits):
        to = lax.rem(me + shift, splits)
        piece = lax.dynamic_slice_in_dim(down_weight, to * width, width, axis=1)
        if shift:
            piece = lax.ppermute(piece, "dp", [(i, (i + shift) % splits) for i in range(splits)])
        pieces.append(piece)
    return pieces


def body(tokens, routes, route_weights, gate_weight, up_weight, down_weight, sketch_basis):
    experts = lax.axis_size("expert")
    token_count, top = routes.shape
    capacity = 2 * token_count * top // experts
    chunks = SLOT_CHUNKS
    slots = capacity // chunks
    width = tokens.shape[1]
    rows = experts * slots

    down = turn_down(down_weight[0], width)
    basis = sketch_basis.T

    own, full, returned = [], [], []
    for chunk, outgoing in enumerate(dispatch(routes, tokens, experts, slots, chunks)):
        arrived = lax.all_to_all(
            outgoing.reshape(experts, slots, width), "expert", split_axis=0, concat_axis=0, tiled=True
        ).reshape(rows, width)
        if chunk == 0:
            arrived, *down = lax.optimization_barrier((arrived, *down))
        wide = lax.all_gather(arrived, "dp", axis=0, tiled=False)
        extra = (basis,) if chunk == 0 else ()
        hidden = hidden_of(wide, gate_weight[0], up_weight[0], extra)
        hidden_all = lax.all_gather(hidden, "dp", axis=0, tiled=False)
        out = output_of(hidden_all, down, rows)
        back = lax.all_to_all(
            out.reshape(experts, slots, width), "expert", split_axis=0, concat_axis=0, tiled=True
        ).reshape(rows, width)
        own.append(hidden)
        full.append(hidden_all)
        returned.append(back)
    gram, projected = moments(full, own, rows, basis.shape[0])
    lower_factor = jnp.linalg.cholesky(gram)
    whitened = jax.scipy.linalg.solve_triangular(lower_factor, projected, lower=True)
    mixed = combine(routes, route_weights, returned, experts, slots)
    return (mixed, whitened[None])


def solution(mesh):
    return jax.shard_map(
        body,
        mesh=mesh,
        in_specs=(
            P("expert", "dp"),
            P("expert", None),
            P("expert", None),
            P("expert", None, "dp"),
            P("expert", None, "dp"),
            P("expert", "dp", None),
            P("dp", None),
        ),
        out_specs=(P("expert", "dp"), P("expert", None, "dp")),
        check_vma=False,
    )
```

```python
import functools

import jax
import jax.numpy as jnp
from jax import lax
from jax.experimental import pallas as pl
from jax.experimental.pallas import tpu as pltpu
from jax.sharding import PartitionSpec as P

ridge_term = 1.0
CUTS = (8, 8)
VMEM = pl.BlockSpec(memory_space=pltpu.VMEM)


def slot_codes(routes, experts):
    tokens, top = routes.shape
    expert_of = lax.broadcasted_iota(jnp.int32, (tokens, experts), 1)
    hits = [(routes[:, k : k + 1] == expert_of).astype(jnp.float32) for k in range(top)]
    hit = functools.reduce(jnp.add, hits)
    row = lax.broadcasted_iota(jnp.int32, (tokens, tokens), 0)
    column = lax.broadcasted_iota(jnp.int32, (tokens, tokens), 1)
    earlier = (row > column).astype(jnp.bfloat16)
    before = jnp.dot(earlier, hit.astype(jnp.bfloat16), preferred_element_type=jnp.float32)
    return hits, jnp.where(hit > 0.0, before, -1.0)


def spread(values, experts, slots):
    expert = lax.broadcasted_iota(jnp.int32, (experts, experts * slots), 0)
    at = lax.broadcasted_iota(jnp.int32, (experts, experts * slots), 1)
    ones = jnp.where(at // slots == expert, 1.0, 0.0).astype(jnp.bfloat16)
    return jnp.dot(values.astype(jnp.bfloat16), ones, preferred_element_type=jnp.float32)


def in_slot(code, experts, slots, start):
    wide = spread(code, experts, slots)
    at = lax.broadcasted_iota(jnp.int32, wide.shape, 1)
    return wide == (lax.rem(at, slots) + start).astype(jnp.float32)


def dispatch_kernel(experts, cuts, routes_ref, tokens_ref, *out_refs):
    _, code = slot_codes(routes_ref[...], experts)
    tokens = tokens_ref[...]
    start = 0
    for slots, out_ref in zip(cuts, out_refs):
        chosen = jnp.where(in_slot(code, experts, slots, start), 1.0, 0.0).T.astype(jnp.bfloat16)
        out_ref[...] = jnp.dot(chosen, tokens, preferred_element_type=jnp.float32).astype(out_ref.dtype)
        start += slots


def dispatch(routes, tokens, experts, cuts):
    width = tokens.shape[1]
    return pl.pallas_call(
        functools.partial(dispatch_kernel, experts, cuts),
        out_shape=[jax.ShapeDtypeStruct((experts * slots, width), tokens.dtype) for slots in cuts],
        in_specs=[VMEM] * 2,
        out_specs=[VMEM] * len(cuts),
        name="dispatch",
    )(routes, tokens)


def combine_kernel(experts, cuts, routes_ref, weights_ref, *refs):
    out_ref = refs[-1]
    hits, code = slot_codes(routes_ref[...], experts)
    weights = weights_ref[...]
    weight = functools.reduce(jnp.add, [h * weights[:, k : k + 1] for k, h in enumerate(hits)])
    high = weight.astype(jnp.bfloat16)
    low = (weight - high.astype(jnp.float32)).astype(jnp.bfloat16)
    total = None
    start = 0
    for slots, row_ref in zip(cuts, refs[:-1]):
        chosen = in_slot(code, experts, slots, start)
        rows = row_ref[...]
        for part in (high, low):
            matrix = jnp.where(chosen, spread(part, experts, slots), 0.0).astype(jnp.bfloat16)
            term = jnp.dot(matrix, rows, preferred_element_type=jnp.float32)
            total = term if total is None else total + term
        start += slots
    out_ref[...] = total.astype(out_ref.dtype)


def combine(routes, weights, rows, experts, cuts):
    return pl.pallas_call(
        functools.partial(combine_kernel, experts, cuts),
        out_shape=jax.ShapeDtypeStruct((routes.shape[0], rows[0].shape[1]), jnp.bfloat16),
        in_specs=[VMEM] * (2 + len(rows)),
        out_specs=VMEM,
        name="combine",
    )(routes, weights, *rows)


def hidden_kernel(me_ref, own_ref, left_ref, right_ref, top_ref, bottom_ref, gate_ref, up_ref, hidden_ref):
    width = own_ref.shape[1]
    parts = gate_ref.shape[0] // width
    step = pl.program_id(0)
    far = jnp.where(step == 0, top_ref[...], bottom_ref[...])
    gate = up = None
    for shift, rows in ((0, own_ref[...]), (parts - 1, left_ref[...]), (1, right_ref[...]), (2, far)):
        at = pl.multiple_of(lax.rem(me_ref[0] + shift, parts) * width, width)
        gate_term = jnp.dot(rows, gate_ref[pl.ds(at, width), :], preferred_element_type=jnp.float32)
        up_term = jnp.dot(rows, up_ref[pl.ds(at, width), :], preferred_element_type=jnp.float32)
        gate = gate_term if gate is None else gate + gate_term
        up = up_term if up is None else up + up_term
    hidden_ref[...] = (gate / (1.0 + jnp.exp(-gate)) * up).astype(hidden_ref.dtype)


def hidden_of(me, ring, gate_weight, up_weight):
    own, left, right, top, bottom = ring
    count, width = own.shape
    depth, units = gate_weight.shape
    half = count // 2
    rows = pl.BlockSpec((half, width), lambda i, me: (i, 0))
    fixed = pl.BlockSpec((half, width), lambda i, me: (0, 0))
    whole = pl.BlockSpec((depth, units), lambda i, me: (0, 0))
    return pl.pallas_call(
        hidden_kernel,
        grid_spec=pltpu.PrefetchScalarGridSpec(
            num_scalar_prefetch=1,
            grid=(2,),
            in_specs=[rows, rows, rows, fixed, fixed, whole, whole],
            out_specs=pl.BlockSpec((half, units), lambda i, me: (i, 0)),
        ),
        out_shape=jax.ShapeDtypeStruct((count, units), jnp.bfloat16),
        cost_estimate=pl.CostEstimate(
            flops=4 * count * depth * units,
            bytes_accessed=2 * depth * (count + 2 * units) + 2 * count * units,
            transcendentals=count * units,
        ),
        compiler_params=pltpu.CompilerParams(vmem_limit_bytes=48 << 20),
        name="hidden",
    )(me, own, left, right, top, bottom, gate_weight, up_weight)


def output_kernel(parts, *refs):
    out_ref, sketch_ref = refs[-2:]
    width = out_ref.shape[1]
    total = None
    for hidden_ref, down_ref in zip(refs[:parts], refs[parts : 2 * parts]):
        term = jnp.dot(hidden_ref[...], down_ref[...], preferred_element_type=jnp.float32)
        total = term if total is None else total + term
    out_ref[...] = total[:, :width].astype(out_ref.dtype)
    sketch_ref[...] = total[:, width:]


def output_of(hidden, down, width):
    count, units = hidden[0].shape
    parts, wide = len(hidden), down[0].shape[1]
    block = count // 2
    return pl.pallas_call(
        functools.partial(output_kernel, parts),
        grid=(count // block,),
        in_specs=[pl.BlockSpec((block, units), lambda i: (i, 0))] * parts
        + [pl.BlockSpec((units, wide), lambda i: (0, 0))] * parts,
        out_specs=[
            pl.BlockSpec((block, width), lambda i: (i, 0)),
            pl.BlockSpec((block, wide - width), lambda i: (i, 0)),
        ],
        out_shape=[
            jax.ShapeDtypeStruct((count, width), jnp.bfloat16),
            jax.ShapeDtypeStruct((count, wide - width), jnp.float32),
        ],
        cost_estimate=pl.CostEstimate(
            flops=2 * parts * count * wide * units,
            bytes_accessed=2 * parts * units * (count + wide) + 4 * count * wide,
            transcendentals=0,
        ),
        compiler_params=pltpu.CompilerParams(vmem_limit_bytes=48 << 20),
        name="output",
    )(*hidden, *down)


def moments_kernel(chunks, *refs):
    gram_ref, project_ref = refs[-2:]
    gram = project = None
    for rows_ref, own_ref in zip(refs[:chunks], refs[chunks : 2 * chunks]):
        rows = rows_ref[...]
        turned = rows.T
        own = own_ref[...].astype(jnp.float32)
        gram_term = jnp.dot(
            turned, rows, precision=lax.Precision.HIGHEST, preferred_element_type=jnp.float32
        )
        project_term = jnp.dot(
            turned, own, precision=lax.Precision.HIGHEST, preferred_element_type=jnp.float32
        )
        gram = gram_term if gram is None else gram + gram_term
        project = project_term if project is None else project + project_term
    size = gram.shape[0]
    row = lax.broadcasted_iota(jnp.int32, (size, size), 0)
    column = lax.broadcasted_iota(jnp.int32, (size, size), 1)
    gram_ref[...] = gram + jnp.where(row == column, ridge_term, 0.0)
    project_ref[...] = project


def moments(rows, own):
    size, units = rows[0].shape[1], own[0].shape[1]
    return pl.pallas_call(
        functools.partial(moments_kernel, len(rows)),
        out_shape=[
            jax.ShapeDtypeStruct((size, size), jnp.float32),
            jax.ShapeDtypeStruct((size, units), jnp.float32),
        ],
        in_specs=[VMEM] * (2 * len(rows)),
        out_specs=[VMEM] * 2,
        compiler_params=pltpu.CompilerParams(vmem_limit_bytes=48 << 20),
        name="moments",
    )(*rows, *own)


def shift_by(value, shift):
    splits = lax.axis_size("dp")
    return lax.ppermute(value, "dp", [(i, (i + shift) % splits) for i in range(splits)])


def turn_down(down_weight, basis, width):
    splits, me = lax.axis_size("dp"), lax.axis_index("dp")
    pieces = []
    for shift in range(splits):
        to = lax.rem(me + shift, splits)
        piece = lax.dynamic_slice_in_dim(down_weight, to * width, width, axis=1)
        piece = jnp.concatenate([piece, basis], axis=1)
        pieces.append(shift_by(piece, shift) if shift else piece)
    return pieces


def around(own):
    half = own.shape[0] // 2
    left, right = shift_by(own, 1), shift_by(own, -1)
    return own, left, right, shift_by(left[:half], 1), shift_by(right[half:], -1)


def body(tokens, routes, route_weights, gate_weight, up_weight, down_weight, sketch_basis):
    experts = lax.axis_size("expert")
    token_count, top = routes.shape
    capacity = 2 * token_count * top // experts
    width = tokens.shape[1]
    me = lax.axis_index("dp").astype(jnp.int32).reshape(1)

    def swap(rows):
        blocks = rows.reshape(experts, rows.shape[0] // experts, width)
        return lax.all_to_all(blocks, "expert", split_axis=0, concat_axis=0, tiled=True).reshape(rows.shape)

    down = turn_down(down_weight[0], sketch_basis, width)
    own, sketch_rows, returned = [], [], []
    for outgoing in dispatch(routes, tokens, experts, CUTS):
        arrived = swap(outgoing)
        if not own:
            arrived, down[1], down[3] = lax.optimization_barrier((arrived, down[1], down[3]))
        hidden = hidden_of(me, around(arrived), gate_weight[0], up_weight[0])
        everywhere = [hidden] + [shift_by(hidden, s) for s in range(1, lax.axis_size("dp"))]
        out, rows = output_of(everywhere, down, width)
        own.append(hidden)
        sketch_rows.append(rows)
        returned.append(swap(out))
    gram, projected = moments(sketch_rows, own)
    lower_factor = jnp.linalg.cholesky(gram)
    whitened = jax.scipy.linalg.solve_triangular(lower_factor, projected, lower=True)
    mixed = combine(routes, route_weights, returned, experts, CUTS)
    return (mixed, whitened[None])


def solution(mesh):
    return jax.shard_map(
        body,
        mesh=mesh,
        in_specs=(
            P("expert", "dp"),
            P("expert", None),
            P("expert", None),
            P("expert", None, "dp"),
            P("expert", None, "dp"),
            P("expert", "dp", None),
            P("dp", None),
        ),
        out_specs=(P("expert", "dp"), P("expert", None, "dp")),
        check_vma=False,
    )
```

```python
import functools

import jax
import jax.numpy as jnp
from jax import lax
from jax.experimental import pallas as pl
from jax.experimental.pallas import tpu as pltpu
from jax.sharding import PartitionSpec as P

ridge_term = 1.0
CUTS = (8, 8)
VMEM = pl.BlockSpec(memory_space=pltpu.VMEM)


def slot_codes(routes, experts):
    tokens, top = routes.shape
    expert_of = lax.broadcasted_iota(jnp.int32, (tokens, experts), 1)
    hits = [(routes[:, k : k + 1] == expert_of).astype(jnp.float32) for k in range(top)]
    hit = functools.reduce(jnp.add, hits)
    row = lax.broadcasted_iota(jnp.int32, (tokens, tokens), 0)
    column = lax.broadcasted_iota(jnp.int32, (tokens, tokens), 1)
    earlier = (row > column).astype(jnp.bfloat16)
    before = jnp.dot(earlier, hit.astype(jnp.bfloat16), preferred_element_type=jnp.float32)
    return hits, jnp.where(hit > 0.0, before, -1.0)


def spread(values, experts, slots):
    expert = lax.broadcasted_iota(jnp.int32, (experts, experts * slots), 0)
    at = lax.broadcasted_iota(jnp.int32, (experts, experts * slots), 1)
    ones = jnp.where(at // slots == expert, 1.0, 0.0).astype(jnp.bfloat16)
    return jnp.dot(values.astype(jnp.bfloat16), ones, preferred_element_type=jnp.float32)


def in_slot(code, experts, slots, start):
    wide = spread(code, experts, slots)
    at = lax.broadcasted_iota(jnp.int32, wide.shape, 1)
    return wide == (lax.rem(at, slots) + start).astype(jnp.float32)


def dispatch_kernel(experts, cuts, routes_ref, tokens_ref, *out_refs):
    _, code = slot_codes(routes_ref[...], experts)
    tokens = tokens_ref[...]
    start = 0
    for slots, out_ref in zip(cuts, out_refs):
        chosen = jnp.where(in_slot(code, experts, slots, start), 1.0, 0.0).T.astype(jnp.bfloat16)
        out_ref[...] = jnp.dot(chosen, tokens, preferred_element_type=jnp.float32).astype(out_ref.dtype)
        start += slots


def dispatch(routes, tokens, experts, cuts):
    width = tokens.shape[1]
    return pl.pallas_call(
        functools.partial(dispatch_kernel, experts, cuts),
        out_shape=[jax.ShapeDtypeStruct((experts * slots, width), tokens.dtype) for slots in cuts],
        in_specs=[VMEM] * 2,
        out_specs=[VMEM] * len(cuts),
        name="dispatch",
    )(routes, tokens)


def combine_kernel(experts, cuts, routes_ref, weights_ref, *refs):
    out_ref = refs[-1]
    hits, code = slot_codes(routes_ref[...], experts)
    weights = weights_ref[...]
    weight = functools.reduce(jnp.add, [h * weights[:, k : k + 1] for k, h in enumerate(hits)])
    high = weight.astype(jnp.bfloat16)
    low = (weight - high.astype(jnp.float32)).astype(jnp.bfloat16)
    total = None
    start = 0
    for slots, row_ref in zip(cuts, refs[:-1]):
        chosen = in_slot(code, experts, slots, start)
        rows = row_ref[...]
        for part in (high, low):
            matrix = jnp.where(chosen, spread(part, experts, slots), 0.0).astype(jnp.bfloat16)
            term = jnp.dot(matrix, rows, preferred_element_type=jnp.float32)
            total = term if total is None else total + term
        start += slots
    out_ref[...] = total.astype(out_ref.dtype)


def combine(routes, weights, rows, experts, cuts):
    return pl.pallas_call(
        functools.partial(combine_kernel, experts, cuts),
        out_shape=jax.ShapeDtypeStruct((routes.shape[0], rows[0].shape[1]), jnp.bfloat16),
        in_specs=[VMEM] * (2 + len(rows)),
        out_specs=VMEM,
        name="combine",
    )(routes, weights, *rows)


def hidden_kernel(me_ref, own_ref, left_ref, right_ref, top_ref, bottom_ref, gate_ref, up_ref, hidden_ref):
    width = own_ref.shape[1]
    parts = gate_ref.shape[0] // width
    step = pl.program_id(0)
    far = jnp.where(step == 0, top_ref[...], bottom_ref[...])
    gate = up = None
    for shift, rows in ((0, own_ref[...]), (parts - 1, left_ref[...]), (1, right_ref[...]), (2, far)):
        at = pl.multiple_of(lax.rem(me_ref[0] + shift, parts) * width, width)
        gate_term = jnp.dot(rows, gate_ref[pl.ds(at, width), :], preferred_element_type=jnp.float32)
        up_term = jnp.dot(rows, up_ref[pl.ds(at, width), :], preferred_element_type=jnp.float32)
        gate = gate_term if gate is None else gate + gate_term
        up = up_term if up is None else up + up_term
    hidden_ref[...] = (gate / (1.0 + jnp.exp(-gate)) * up).astype(hidden_ref.dtype)


def hidden_of(me, ring, gate_weight, up_weight):
    own, left, right, top, bottom = ring
    count, width = own.shape
    depth, units = gate_weight.shape
    half = count // 2
    rows = pl.BlockSpec((half, width), lambda i, me: (i, 0))
    fixed = pl.BlockSpec((half, width), lambda i, me: (0, 0))
    whole = pl.BlockSpec((depth, units), lambda i, me: (0, 0))
    return pl.pallas_call(
        hidden_kernel,
        grid_spec=pltpu.PrefetchScalarGridSpec(
            num_scalar_prefetch=1,
            grid=(2,),
            in_specs=[rows, rows, rows, fixed, fixed, whole, whole],
            out_specs=pl.BlockSpec((half, units), lambda i, me: (i, 0)),
        ),
        out_shape=jax.ShapeDtypeStruct((count, units), jnp.bfloat16),
        cost_estimate=pl.CostEstimate(
            flops=4 * count * depth * units,
            bytes_accessed=2 * depth * (count + 2 * units) + 2 * count * units,
            transcendentals=count * units,
        ),
        compiler_params=pltpu.CompilerParams(vmem_limit_bytes=48 << 20),
        name="hidden",
    )(me, own, left, right, top, bottom, gate_weight, up_weight)


def output_kernel(parts, *refs):
    out_ref, sketch_ref = refs[-2:]
    width = out_ref.shape[1]
    total = None
    for hidden_ref, down_ref in zip(refs[:parts], refs[parts : 2 * parts]):
        term = jnp.dot(hidden_ref[...], down_ref[...], preferred_element_type=jnp.float32)
        total = term if total is None else total + term
    out_ref[...] = total[:, :width].astype(out_ref.dtype)
    sketch_ref[...] = total[:, width:]


def output_of(hidden, down, width):
    count, units = hidden[0].shape
    parts, wide = len(hidden), down[0].shape[1]
    block = count // 2
    return pl.pallas_call(
        functools.partial(output_kernel, parts),
        grid=(count // block,),
        in_specs=[pl.BlockSpec((block, units), lambda i: (i, 0))] * parts
        + [pl.BlockSpec((units, wide), lambda i: (0, 0))] * parts,
        out_specs=[
            pl.BlockSpec((block, width), lambda i: (i, 0)),
            pl.BlockSpec((block, wide - width), lambda i: (i, 0)),
        ],
        out_shape=[
            jax.ShapeDtypeStruct((count, width), jnp.bfloat16),
            jax.ShapeDtypeStruct((count, wide - width), jnp.float32),
        ],
        cost_estimate=pl.CostEstimate(
            flops=2 * parts * count * wide * units,
            bytes_accessed=2 * parts * units * (count + wide) + 4 * count * wide,
            transcendentals=0,
        ),
        compiler_params=pltpu.CompilerParams(vmem_limit_bytes=48 << 20),
        name="output",
    )(*hidden, *down)


def moments_kernel(chunks, *refs):
    gram_ref, project_ref = refs[-2:]
    gram = project = None
    for rows_ref, own_ref in zip(refs[:chunks], refs[chunks : 2 * chunks]):
        rows = rows_ref[...]
        turned = rows.T
        own = own_ref[...].astype(jnp.float32)
        gram_term = jnp.dot(
            turned, rows, precision=lax.Precision.HIGHEST, preferred_element_type=jnp.float32
        )
        project_term = jnp.dot(
            turned, own, precision=lax.Precision.HIGHEST, preferred_element_type=jnp.float32
        )
        gram = gram_term if gram is None else gram + gram_term
        project = project_term if project is None else project + project_term
    size = gram.shape[0]
    row = lax.broadcasted_iota(jnp.int32, (size, size), 0)
    column = lax.broadcasted_iota(jnp.int32, (size, size), 1)
    gram_ref[...] = gram + jnp.where(row == column, ridge_term, 0.0)
    project_ref[...] = project


def moments(rows, own):
    size, units = rows[0].shape[1], own[0].shape[1]
    return pl.pallas_call(
        functools.partial(moments_kernel, len(rows)),
        out_shape=[
            jax.ShapeDtypeStruct((size, size), jnp.float32),
            jax.ShapeDtypeStruct((size, units), jnp.float32),
        ],
        in_specs=[VMEM] * (2 * len(rows)),
        out_specs=[VMEM] * 2,
        compiler_params=pltpu.CompilerParams(vmem_limit_bytes=48 << 20),
        name="moments",
    )(*rows, *own)


def shift_by(value, shift):
    splits = lax.axis_size("dp")
    return lax.ppermute(value, "dp", [(i, (i + shift) % splits) for i in range(splits)])


def after_kernel(*refs):
    pass


def after(value, *others):
    anywhere = pl.BlockSpec(memory_space=pl.ANY)
    return pl.pallas_call(
        after_kernel,
        out_shape=jax.ShapeDtypeStruct(value.shape, value.dtype),
        in_specs=[anywhere] * (1 + len(others)),
        out_specs=anywhere,
        input_output_aliases={0: 0},
        name="after",
    )(value, *others)


def turn_down(down_weight, basis, width):
    splits, me = lax.axis_size("dp"), lax.axis_index("dp")
    pieces = []
    for shift in range(splits):
        to = lax.rem(me + shift, splits)
        piece = lax.dynamic_slice_in_dim(down_weight, to * width, width, axis=1)
        piece = jnp.concatenate([piece, basis], axis=1)
        pieces.append(shift_by(piece, shift) if shift else piece)
    return pieces


def around(own):
    half = own.shape[0] // 2
    left, right = shift_by(own, 1), shift_by(own, -1)
    return own, left, right, shift_by(left[:half], 1), shift_by(right[half:], -1)


def body(tokens, routes, route_weights, gate_weight, up_weight, down_weight, sketch_basis):
    experts = lax.axis_size("expert")
    token_count, top = routes.shape
    capacity = 2 * token_count * top // experts
    width = tokens.shape[1]
    me = lax.axis_index("dp").astype(jnp.int32).reshape(1)

    def swap(rows):
        blocks = rows.reshape(experts, rows.shape[0] // experts, width)
        return lax.all_to_all(blocks, "expert", split_axis=0, concat_axis=0, tiled=True).reshape(rows.shape)

    down = turn_down(down_weight[0], sketch_basis, width)
    own, sketch_rows, returned = [], [], []
    for outgoing in dispatch(routes, tokens, experts, CUTS):
        arrived = swap(outgoing if not own else after(outgoing, arrived))
        if not own:
            arrived = after(arrived, down[1], down[3])
        hidden = hidden_of(me, around(arrived), gate_weight[0], up_weight[0])
        everywhere = [hidden] + [shift_by(hidden, s) for s in range(1, lax.axis_size("dp"))]
        out, rows = output_of(everywhere, down, width)
        own.append(hidden)
        sketch_rows.append(rows)
        returned.append(swap(out))
    gram, projected = moments(sketch_rows, own)
    lower_factor = jnp.linalg.cholesky(gram)
    whitened = jax.scipy.linalg.solve_triangular(lower_factor, projected, lower=True)
    mixed = combine(routes, route_weights, returned, experts, CUTS)
    return (mixed, whitened[None])


def solution(mesh):
    return jax.shard_map(
        body,
        mesh=mesh,
        in_specs=(
            P("expert", "dp"),
            P("expert", None),
            P("expert", None),
            P("expert", None, "dp"),
            P("expert", None, "dp"),
            P("expert", "dp", None),
            P("dp", None),
        ),
        out_specs=(P("expert", "dp"), P("expert", None, "dp")),
        check_vma=False,
    )
```

```python
import functools

import jax
import jax.numpy as jnp
from jax import lax
from jax.experimental import pallas as pl
from jax.experimental.pallas import tpu as pltpu
from jax.sharding import PartitionSpec as P

ridge_term = 1.0
CUTS = (8, 8)
VMEM = pl.BlockSpec(memory_space=pltpu.VMEM)

def slot_codes(routes, experts):
    tokens, top = routes.shape
    expert_of = lax.broadcasted_iota(jnp.int32, (tokens, experts), 1)
    hits = [(routes[:, k : k + 1] == expert_of).astype(jnp.float32) for k in range(top)]
    hit = functools.reduce(jnp.add, hits)
    row = lax.broadcasted_iota(jnp.int32, (tokens, tokens), 0)
    column = lax.broadcasted_iota(jnp.int32, (tokens, tokens), 1)
    earlier = (row > column).astype(jnp.bfloat16)
    before = jnp.dot(earlier, hit.astype(jnp.bfloat16), preferred_element_type=jnp.float32)
    return hits, jnp.where(hit > 0.0, before, -1.0)

def spread(values, experts, slots):
    expert = lax.broadcasted_iota(jnp.int32, (experts, experts * slots), 0)
    at = lax.broadcasted_iota(jnp.int32, (experts, experts * slots), 1)
    ones = jnp.where(at // slots == expert, 1.0, 0.0).astype(jnp.bfloat16)
    return jnp.dot(values.astype(jnp.bfloat16), ones, preferred_element_type=jnp.float32)

def in_slot(code, experts, slots, start):
    wide = spread(code, experts, slots)
    at = lax.broadcasted_iota(jnp.int32, wide.shape, 1)
    return wide == (lax.rem(at, slots) + start).astype(jnp.float32)

def dispatch_kernel(experts, cuts, routes_ref, tokens_ref, *out_refs):
    _, code = slot_codes(routes_ref[...], experts)
    tokens = tokens_ref[...]
    start = 0
    for slots, out_ref in zip(cuts, out_refs):
        chosen = jnp.where(in_slot(code, experts, slots, start), 1.0, 0.0).T.astype(jnp.bfloat16)
        out_ref[...] = jnp.dot(chosen, tokens, preferred_element_type=jnp.float32).astype(out_ref.dtype)
        start += slots

def dispatch(routes, tokens, experts, cuts):
    width = tokens.shape[1]
    return pl.pallas_call(
        functools.partial(dispatch_kernel, experts, cuts),
        out_shape=[jax.ShapeDtypeStruct((experts * slots, width), tokens.dtype) for slots in cuts],
        in_specs=[VMEM] * 2,
        out_specs=[VMEM] * len(cuts),
        name="dispatch",
    )(routes, tokens)

def combine_kernel(experts, cuts, routes_ref, weights_ref, *refs):
    out_ref = refs[-1]
    hits, code = slot_codes(routes_ref[...], experts)
    weights = weights_ref[...]
    weight = functools.reduce(jnp.add, [h * weights[:, k : k + 1] for k, h in enumerate(hits)])
    high = weight.astype(jnp.bfloat16)
    low = (weight - high.astype(jnp.float32)).astype(jnp.bfloat16)
    total = None
    start = 0
    for slots, row_ref in zip(cuts, refs[:-1]):
        chosen = in_slot(code, experts, slots, start)
        rows = row_ref[...]
        for part in (high, low):
            matrix = jnp.where(chosen, spread(part, experts, slots), 0.0).astype(jnp.bfloat16)
            term = jnp.dot(matrix, rows, preferred_element_type=jnp.float32)
            total = term if total is None else total + term
        start += slots
    out_ref[...] = total.astype(out_ref.dtype)

def combine(routes, weights, rows, experts, cuts):
    return pl.pallas_call(
        functools.partial(combine_kernel, experts, cuts),
        out_shape=jax.ShapeDtypeStruct((routes.shape[0], rows[0].shape[1]), jnp.bfloat16),
        in_specs=[VMEM] * (2 + len(rows)),
        out_specs=VMEM,
        name="combine",
    )(routes, weights, *rows)

def hidden_kernel(me_ref, own_ref, left_ref, right_ref, top_ref, bottom_ref, gate_ref, up_ref, hidden_ref):
    width = own_ref.shape[1]
    parts = gate_ref.shape[0] // width
    step = pl.program_id(0)
    far = jnp.where(step == 0, top_ref[...], bottom_ref[...])
    gate = up = None
    for shift, rows in ((0, own_ref[...]), (parts - 1, left_ref[...]), (1, right_ref[...]), (2, far)):
        at = pl.multiple_of(lax.rem(me_ref[0] + shift, parts) * width, width)
        gate_term = jnp.dot(rows, gate_ref[pl.ds(at, width), :], preferred_element_type=jnp.float32)
        up_term = jnp.dot(rows, up_ref[pl.ds(at, width), :], preferred_element_type=jnp.float32)
        gate = gate_term if gate is None else gate + gate_term
        up = up_term if up is None else up + up_term
    hidden_ref[...] = (gate / (1.0 + jnp.exp(-gate)) * up).astype(hidden_ref.dtype)

def hidden_of(me, ring, gate_weight, up_weight):
    own, left, right, top, bottom = ring
    count, width = own.shape
    depth, units = gate_weight.shape
    half = count // 2
    rows = pl.BlockSpec((half, width), lambda i, me: (i, 0))
    fixed = pl.BlockSpec((half, width), lambda i, me: (0, 0))
    whole = pl.BlockSpec((depth, units), lambda i, me: (0, 0))
    return pl.pallas_call(
        hidden_kernel,
        grid_spec=pltpu.PrefetchScalarGridSpec(
            num_scalar_prefetch=1,
            grid=(2,),
            in_specs=[rows, rows, rows, fixed, fixed, whole, whole],
            out_specs=pl.BlockSpec((half, units), lambda i, me: (i, 0)),
        ),
        out_shape=jax.ShapeDtypeStruct((count, units), jnp.bfloat16),
        cost_estimate=pl.CostEstimate(
            flops=4 * count * depth * units,
            bytes_accessed=2 * depth * (count + 2 * units) + 2 * count * units,
            transcendentals=count * units,
        ),
        compiler_params=pltpu.CompilerParams(vmem_limit_bytes=48 << 20),
        name="hidden",
    )(me, own, left, right, top, bottom, gate_weight, up_weight)

def output_kernel(parts, *refs):
    out_ref, sketch_ref = refs[-2:]
    width = out_ref.shape[1]
    total = None
    for hidden_ref, down_ref in zip(refs[:parts], refs[parts : 2 * parts]):
        term = jnp.dot(hidden_ref[...], down_ref[...], preferred_element_type=jnp.float32)
        total = term if total is None else total + term
    out_ref[...] = total[:, :width].astype(out_ref.dtype)
    sketch_ref[...] = total[:, width:]

def output_of(hidden, down, width):
    count, units = hidden[0].shape
    parts, wide = len(hidden), down[0].shape[1]
    block = count // 2
    return pl.pallas_call(
        functools.partial(output_kernel, parts),
        grid=(count // block,),
        in_specs=[pl.BlockSpec((block, units), lambda i: (i, 0))] * parts
        + [pl.BlockSpec((units, wide), lambda i: (0, 0))] * parts,
        out_specs=[
            pl.BlockSpec((block, width), lambda i: (i, 0)),
            pl.BlockSpec((block, wide - width), lambda i: (i, 0)),
        ],
        out_shape=[
            jax.ShapeDtypeStruct((count, width), jnp.bfloat16),
            jax.ShapeDtypeStruct((count, wide - width), jnp.float32),
        ],
        cost_estimate=pl.CostEstimate(
            flops=2 * parts * count * wide * units,
            bytes_accessed=2 * parts * units * (count + wide) + 4 * count * wide,
            transcendentals=0,
        ),
        compiler_params=pltpu.CompilerParams(vmem_limit_bytes=48 << 20),
        name="output",
    )(*hidden, *down)

def moments_kernel(chunks, *refs):
    gram_ref, project_ref = refs[-2:]
    gram = project = None
    for rows_ref, own_ref in zip(refs[:chunks], refs[chunks : 2 * chunks]):
        rows = rows_ref[...]
        turned = rows.T
        own = own_ref[...].astype(jnp.float32)
        gram_term = jnp.dot(
            turned, rows, precision=lax.Precision.HIGHEST, preferred_element_type=jnp.float32
        )
        project_term = jnp.dot(
            turned, own, precision=lax.Precision.HIGHEST, preferred_element_type=jnp.float32
        )
        gram = gram_term if gram is None else gram + gram_term
        project = project_term if project is None else project + project_term
    size = gram.shape[0]
    row = lax.broadcasted_iota(jnp.int32, (size, size), 0)
    column = lax.broadcasted_iota(jnp.int32, (size, size), 1)
    gram_ref[...] = gram + jnp.where(row == column, ridge_term, 0.0)
    project_ref[...] = project

def moments(rows, own):
    size, units = rows[0].shape[1], own[0].shape[1]
    return pl.pallas_call(
        functools.partial(moments_kernel, len(rows)),
        out_shape=[
            jax.ShapeDtypeStruct((size, size), jnp.float32),
            jax.ShapeDtypeStruct((size, units), jnp.float32),
        ],
        in_specs=[VMEM] * (2 * len(rows)),
        out_specs=[VMEM] * 2,
        compiler_params=pltpu.CompilerParams(vmem_limit_bytes=48 << 20),
        name="moments",
    )(*rows, *own)

def shift_by(value, shift):
    splits = lax.axis_size("dp")
    return lax.ppermute(value, "dp", [(i, (i + shift) % splits) for i in range(splits)])

def after_kernel(*refs):
    pass

def after(value, *others):
    anywhere = pl.BlockSpec(memory_space=pl.ANY)
    return pl.pallas_call(
        after_kernel,
        out_shape=jax.ShapeDtypeStruct(value.shape, value.dtype),
        in_specs=[anywhere] * (1 + len(others)),
        out_specs=anywhere,
        input_output_aliases={0: 0},
        name="after",
    )(value, *others)

def turn_down(down_weight, basis, width):
    splits, me = lax.axis_size("dp"), lax.axis_index("dp")
    half = down_weight.shape[0] // 2

    def piece(shift, rows):
        at = lax.rem(me + shift, splits) * width
        cut = lax.dynamic_slice(down_weight, (rows.start, at), (rows.stop - rows.start, width))
        return jnp.concatenate([cut, basis[rows]], axis=1)

    every, upper, lower = slice(0, 2 * half), slice(0, half), slice(half, 2 * half)
    onward = shift_by(jnp.concatenate([piece(2, upper), piece(1, every)]), 1)
    backward = shift_by(jnp.concatenate([piece(2, lower), piece(splits - 1, every)]), -1)
    far = jnp.concatenate([shift_by(onward[:half], 1), shift_by(backward[:half], -1)])
    return [piece(0, every), onward[half:], far, backward[half:]], (onward, backward)

def around(own):
    half = own.shape[0] // 2
    left, right = shift_by(own, 1), shift_by(own, -1)
    return own, left, right, shift_by(left[:half], 1), shift_by(right[half:], -1)

def body(tokens, routes, route_weights, gate_weight, up_weight, down_weight, sketch_basis):
    experts = lax.axis_size("expert")
    token_count, top = routes.shape
    capacity = 2 * token_count * top // experts
    width = tokens.shape[1]
    me = lax.axis_index("dp").astype(jnp.int32).reshape(1)

    def swap(rows):
        blocks = rows.reshape(experts, rows.shape[0] // experts, width)
        return lax.all_to_all(blocks, "expert", split_axis=0, concat_axis=0, tiled=True).reshape(rows.shape)

    down, near = turn_down(down_weight[0], sketch_basis, width)
    first, second = dispatch(routes, tokens, experts, CUTS)
    gate, up = gate_weight[0], up_weight[0]

    def spread_hidden(hidden):
        return [hidden] + [shift_by(hidden, s) for s in range(1, lax.axis_size("dp"))]

    rows0 = swap(first)
    rows1 = swap(after(second, rows0))
    rows0 = after(rows0, *near)
    ring0 = around(rows0)
    ring1 = around(rows1)
    ring0 = (after(ring0[0], rows1),) + ring0[1:]
    hidden0 = hidden_of(me, ring0, gate, up)

    hidden1 = hidden_of(me, ring1, gate, up)
    everywhere0 = spread_hidden(hidden0)

    out0, sketch0 = output_of(everywhere0, down, width)
    back0 = swap(out0)
    everywhere1 = spread_hidden(hidden1)

    out1, sketch1 = output_of(everywhere1, down, width)
    back1 = swap(out1)
    own, sketch_rows, returned = [hidden0, hidden1], [sketch0, sketch1], [back0, back1]
    gram, projected = moments(sketch_rows, own)
    lower_factor = jnp.linalg.cholesky(gram)
    whitened = jax.scipy.linalg.solve_triangular(lower_factor, projected, lower=True)
    mixed = combine(routes, route_weights, returned, experts, CUTS)
    return (mixed, whitened[None])

def solution(mesh):
    return jax.shard_map(
        body,
        mesh=mesh,
        in_specs=(
            P("expert", "dp"),
            P("expert", None),
            P("expert", None),
            P("expert", None, "dp"),
            P("expert", None, "dp"),
            P("expert", "dp", None),
            P("dp", None),
        ),
        out_specs=(P("expert", "dp"), P("expert", None, "dp")),
        check_vma=False,
    )
```
